32 devices in a mesh: row: 4 (over x, core), col: 8 (over z, y).
Axes of the slice: x: 2, y: 2, z: 4, core: 2. Of those that a mesh axis runs over, the one named last changes fastest.
Arguments:
- depth: float32 [3072, 8192], P('row', 'col'), may hold values from 0.05 to 2
- ground: float32 [3072, 8192], P('row', 'col'), may hold values from -4 to 4
- flow_rows: float32 [3072, 8192], P('row', 'col'), may hold values from -3 to 3
- flow_cols: float32 [3072, 8192], P('row', 'col'), may hold values from -3 to 3
- wet_tiles: int32 [4, 8], P('row', 'col'), may hold values 0 or 1
- inlet_cell: int32 [4, 8, 4096], P('row', 'col'), may hold values from 0 to 786431
- inlet_node: int32 [4, 8, 4096], P('row', 'col'), may hold values from 0 to 2047
- inlet_coef: float32 [4, 8, 4096], P('row', 'col'), may hold values from 0.05 to 0.5
- shift_rows: int32 [4, 8], P('row', 'col'), may hold values from 0 to 2, as said below
- shift_cols: int32 [4, 8], P('row', 'col'), may hold values from 0 to 2, as said below
Outputs:
- depth_out: float32 [3072, 8192], P('row', 'col')
- rows_out: float32 [3072, 8192], P('row', 'col')
- cols_out: float32 [3072, 8192], P('row', 'col')
- node_inflow: float32 [2048], P(('row', 'col'))
- moved_rows: float32 [3, 1024, 8192], P(None, 'row', 'col')
- moved_cols: float32 [3, 3072, 2048], P(None, 'row', 'col')
The draws below stay inside these ranges and needn't reach their ends.
Inputs may be any that keep to these rules, and one draw needn't show every extreme that they name: `shift_rows`: some tile reaches 2 in every draw. `shift_cols`: some tile reaches 2 in every draw.
All inputs are finite; a program needn't handle non-finite values. No bound on the sum of `wet_tiles` on one device may be relied on, other than what follows from the above.
Results may differ from the reference program's by a relative error of at most 0.00002.
Values sent between devices are 32-bit elements; how exact they have to be, the bound alone decides.
A program may use at most 128 MiB of HBM per device.

```python
import math
import jax
import jax.numpy as jnp

CX = 768
CY = 1024
STEPS = 3
BLOCK = 128
MAX_BLOCKS = 2
INLET_DEV = 4096
NX = 3072
NY = 8192
NODES = 2048
N_ROW = 4
N_COL = 8


def pick_counts(key):
    total = N_ROW * N_COL
    base = jax.random.randint(key, (total,), 0, MAX_BLOCKS + 1)
    spot = jax.random.randint(jax.random.fold_in(key, 7), (), 0, total)
    return base.at[spot].set(MAX_BLOCKS).reshape(N_ROW, N_COL).astype(jnp.int32)


def draw_shift_rows(key, part):
    return pick_counts(jax.random.fold_in(key, 1))


def draw_shift_cols(key, part):
    return pick_counts(jax.random.fold_in(key, 2))


def plant(result, stream_key, least, largest):
    longest = result.shape.index(max(result.shape))
    spots = []
    for shift in (0, 1):
        where = [jax.random.randint(jax.random.fold_in(stream_key, axis), (), 0, length) for axis, length in enumerate(result.shape)]
        where[longest] = (where[longest] + shift) % result.shape[longest]
        spots.append(tuple(where))
    return result.at[spots[0]].set(least).at[spots[1]].set(largest)


def level_of(stream_key, extent, cuts, low, top_value):
    def one(position, parts):
        draws = jax.random.uniform(jax.random.fold_in(jax.random.fold_in(stream_key, 6), position), (parts,), jnp.float32, low / len(cuts), top_value / len(cuts))
        return jnp.repeat(jnp.exp(draws), extent[position] // parts).reshape((-1,) + (1,) * (len(extent) - position - 1))

    gain = one(*cuts[0])
    for cut in cuts[1:]:
        gain = gain * one(*cut)
    return gain


def normal_values(key, dims, width, most, shards=(), kind=jnp.bfloat16):
    result = width * jax.random.normal(key, dims, jnp.float32)
    if shards:
        result = result * level_of(key, dims, shards, -0.22, 0.18)
    return jnp.clip(result, -most, most).astype(kind)


def setup_inputs(seed: int = 0) -> dict:
    keys = jax.random.split(jax.random.key(seed), 11)
    depth = jnp.clip(jnp.exp(math.log(2.0) - 3.6888794 * jax.random.uniform(keys[0], (NX, NY), jnp.float32) ** level_of(keys[0], (NX, NY), ((0, 4), (1, 8)), -0.2, 0.2)), 0.05, 2.0)
    ground = normal_values(keys[1], (NX, NY), 0.3, 4.0, ((0, 4), (1, 8)), jnp.float32)
    flow_rows = normal_values(keys[2], (NX, NY), 0.2, 3.0, ((0, 4), (1, 8)), jnp.float32)
    flow_cols = normal_values(keys[3], (NX, NY), 0.2, 3.0, ((0, 4), (1, 8)), jnp.float32)
    wet_tiles = plant((jax.random.randint(keys[4], (N_ROW, N_COL), 0, 4) < 3).astype(jnp.int32), jax.random.fold_in(keys[4], 1), 0, 1)
    inlet_cell = plant(jax.random.randint(keys[5], (N_ROW, N_COL, INLET_DEV), 0, CX * CY), jax.random.fold_in(keys[5], 1), 0, (CX * CY) - 1).astype(jnp.int32)
    inlet_node = plant(jax.random.randint(keys[6], (N_ROW, N_COL, INLET_DEV), 0, NODES), jax.random.fold_in(keys[6], 1), 0, NODES - 1).astype(jnp.int32)
    inlet_coef = jnp.clip(jnp.exp(math.log(0.5) - 2.3025851 * jax.random.uniform(keys[7], (N_ROW, N_COL, INLET_DEV), jnp.float32) ** level_of(keys[7], (N_ROW, N_COL, INLET_DEV), ((0, 4), (1, 8)), -0.2, 0.2)), 0.05, 0.5)
    shift_rows = draw_shift_rows(jax.random.fold_in(keys[10], 71), 0)
    shift_cols = draw_shift_cols(jax.random.fold_in(keys[10], 71), 0)
    return dict(depth=depth, ground=ground, flow_rows=flow_rows, flow_cols=flow_cols, wet_tiles=wet_tiles, inlet_cell=inlet_cell, inlet_node=inlet_node, inlet_coef=inlet_coef, shift_rows=shift_rows, shift_cols=shift_cols)


gravity = 9.81
time_step = 0.1
friction = 0.0025
depth_floor = 0.25


def face_update(flow, eta, eta_next, ground, ground_next):
    top = jnp.maximum(eta, eta_next) - jnp.maximum(ground, ground_next)
    face_depth = jnp.maximum(top, 0.0)
    floored = jnp.maximum(face_depth, depth_floor)
    pushed = flow - gravity * time_step * face_depth * (eta_next - eta)
    return pushed / (1.0 + gravity * time_step * friction * jnp.abs(flow) / floored ** (7.0 / 3.0))


def reference(depth, ground, flow_rows, flow_cols, wet_tiles, inlet_cell, inlet_node, inlet_coef, shift_rows, shift_cols):
    wet = jnp.repeat(jnp.repeat(wet_tiles > 0, CX, axis=0), CY, axis=1)
    ground_pad = jnp.pad(ground, 1)
    for step in range(STEPS):
        eta_pad = jnp.pad(depth, 1) + ground_pad
        eta = eta_pad[1:-1, 1:-1]
        new_rows = face_update(flow_rows, eta, eta_pad[2:, 1:-1], ground, ground_pad[2:, 1:-1])
        new_cols = face_update(flow_cols, eta, eta_pad[1:-1, 2:], ground, ground_pad[1:-1, 2:])
        new_rows = jnp.where(wet, new_rows, flow_rows)
        new_cols = jnp.where(wet, new_cols, flow_cols)
        rows_pad = jnp.pad(new_rows, 1)
        cols_pad = jnp.pad(new_cols, 1)
        new_depth = depth + time_step * (rows_pad[:-2, 1:-1] - new_rows + cols_pad[1:-1, :-2] - new_cols)
        depth = jnp.where(wet, new_depth, depth)
        flow_rows, flow_cols = new_rows, new_cols
    tile_row = jnp.arange(N_ROW).astype(jnp.int32)[:, None, None]
    tile_col = jnp.arange(N_COL).astype(jnp.int32)[None, :, None]
    global_row = tile_row * CX + inlet_cell // CY
    global_col = tile_col * CY + inlet_cell % CY
    captured = inlet_coef * jnp.maximum(depth[global_row, global_col], 0.0)
    node_inflow = jax.ops.segment_sum(captured.reshape(-1), inlet_node.reshape(-1), num_segments=NODES)
    state = jnp.stack([depth, flow_rows, flow_cols])
    span = MAX_BLOCKS * BLOCK
    offsets = jnp.arange(span).astype(jnp.int32)
    by_rows = state.reshape(3, N_ROW, CX, NY)[:, :, CX - span:, :]
    keep_rows = jnp.repeat(shift_rows, CY, axis=1)
    mask_rows = offsets[None, :, None] >= (MAX_BLOCKS - keep_rows[:, None, :]) * BLOCK
    by_rows = jnp.where(mask_rows[None], by_rows, 0.0)
    by_rows = jnp.concatenate([jnp.zeros_like(by_rows[:, :1]), by_rows[:, :-1]], axis=1)
    moved_rows = by_rows.reshape(3, N_ROW * span, NY)
    by_cols = state.reshape(3, NX, N_COL, CY)[:, :, :, CY - span:]
    keep_cols = jnp.repeat(shift_cols, CX, axis=0)
    mask_cols = offsets[None, None, :] >= (MAX_BLOCKS - keep_cols[:, :, None]) * BLOCK
    by_cols = jnp.where(mask_cols[None], by_cols, 0.0)
    by_cols = jnp.concatenate([jnp.zeros_like(by_cols[:, :, :1]), by_cols[:, :, :-1]], axis=2)
    moved_cols = by_cols.reshape(3, NX, N_COL * span)
    return depth, flow_rows, flow_cols, node_inflow, moved_rows, moved_cols
```

```python
import functools

import jax
import jax.numpy as jnp
from jax import lax
from jax.experimental import pallas as pl
from jax.experimental.pallas import tpu as pltpu
from jax.sharding import PartitionSpec as P

STEPS = 3
BLOCK = 128
MAX_BLOCKS = 2
NODE_DEV = 64
LANES = 128
SUB = 8
EDGE = 4


gravity = 9.81
time_step = 0.1
friction = 0.0025
depth_floor = 0.25


def passed_along(value, axis, steps):
    count = lax.axis_size(axis)
    leading, last = (max(0, -steps), min(count, count - steps))
    return lax.ppermute(value, axis, [(source, source + steps) for source in range(leading, last)])


def face_update(flow, eta, eta_next, top_ground):
    face_depth = jnp.maximum(jnp.maximum(eta, eta_next) - top_ground, 0.0)
    floored = jnp.maximum(face_depth, depth_floor)
    drag = (gravity * time_step * friction) * jnp.abs(flow) * jnp.exp((-7.0 / 3.0) * jnp.log(floored))
    pushed = flow - (gravity * time_step) * face_depth * (eta_next - eta)
    return pushed / (1.0 + drag)


def steps_kernel(cs, row0, rows, kind, *refs):
    depth, ground, frow, fcol, top, bottom, side, wet, shift = refs[:9]
    if kind == "all":
        outs, scratch = refs[9:12], refs[12:]
    else:
        outs, scratch = refs[9:10], refs[10:]
    d, g, f, c, w8, zc, zero, in_sem, side_sem, out_sem = scratch
    n = len(cs)
    high = rows - row0 + 32
    arrays = ((depth, d), (ground, g), (frow, f), (fcol, c))
    copies = []
    for a, (src, dst) in enumerate(arrays):
        for i, slab in enumerate(cs[:-1]):
            copies.append(pltpu.make_async_copy(
                src.at[pl.ds(row0, rows - row0), pl.ds(slab * LANES, LANES)],
                dst.at[pl.ds(i * high + 16, rows - row0)], in_sem.at[a, i]))
    skip = 0 if row0 == 0 else 16
    for a, dst in enumerate((d, g, f, c, w8)):
        base = (n - 1) * high if a < 4 else 0
        copies.append(pltpu.make_async_copy(
            side.at[a, pl.ds(row0 + skip, high - skip)], dst.at[pl.ds(base + skip, high - skip)], side_sem.at[a]))
    for copy in copies:
        copy.start()
    blank = jnp.zeros((SUB, LANES), jnp.float32)
    for a, (_, dst) in enumerate(arrays):
        for i in range(n):
            if i == n - 1 and row0 == 0:
                continue
            dst[pl.ds(i * high, SUB), :] = blank
            if i == n - 1:
                dst[pl.ds(i * high + 8, SUB), :] = blank
                continue
            lanes = pl.ds(cs[i] * LANES, LANES)
            dst[pl.ds(i * high + 8, SUB), :] = top[a, :, lanes] if row0 == 0 else blank
            dst[pl.ds(i * high + high - 16, SUB), :] = bottom[a, :, lanes]
            dst[pl.ds(i * high + high - 8, SUB), :] = blank
    if kind != "all":
        zero[...] = jnp.zeros_like(zero)
    for copy in copies:
        copy.wait()

    lane = lax.broadcasted_iota(jnp.int32, (SUB, LANES), 1)
    at_last, at_first = lane == LANES - 1, lane == 0

    def rightward(vals):
        rolled = [pltpu.roll(v, LANES - 1, 1) for v in vals]
        return [jnp.where(at_last, rolled[(i + 1) % n], rolled[i]) for i in range(n)]

    def leftward(vals):
        rolled = [pltpu.roll(v, 1, 1) for v in vals]
        return [jnp.where(at_first, rolled[(i - 1) % n], rolled[i]) for i in range(n)]

    first = 1 if row0 == 0 else 2
    last = high // SUB - 2
    sizes = [i * high for i in range(n)]

    def bed(b, carry):
        r = pl.multiple_of(b * SUB, SUB)
        vals = [g[pl.ds(s + r, SUB), :] for s in sizes]
        for s, v, q in zip(sizes, vals, rightward(vals)):
            zc[pl.ds(s + r, SUB), :] = jnp.maximum(v, q)
        return carry

    lax.fori_loop(first, last + 1, bed, 0)
    active = jnp.broadcast_to(wet[0, 0], (SUB, LANES)) > 0
    top_active = top[4, :, pl.ds(0, LANES)] > 0.0
    bottom_active = bottom[4, :, pl.ds(0, LANES)] > 0.0

    def block(b, mask):
        r = b * SUB if isinstance(b, int) else pl.multiple_of(b * SUB, SUB)
        masks = [mask] * (n - 1) + [w8[pl.ds(r, SUB), :] > 0.0]
        depths = [d[pl.ds(s + r, SUB), :] for s in sizes]
        grounds = [g[pl.ds(s + r, SUB), :] for s in sizes]
        eta = [x + y for x, y in zip(depths, grounds)]
        right = rightward(eta)
        cols = []
        for i, s in enumerate(sizes):
            old = c[pl.ds(s + r, SUB), :]
            new = face_update(old, eta[i], right[i], zc[pl.ds(s + r, SUB), :])
            new = jnp.where(masks[i], new, old)
            c[pl.ds(s + r, SUB), :] = new
            cols.append(new)
        before = leftward(cols)
        for i, s in enumerate(sizes):
            below = g[pl.ds(s + r + 1, SUB), :]
            old = f[pl.ds(s + r, SUB), :]
            eta_below = d[pl.ds(s + r + 1, SUB), :] + below
            new = face_update(old, eta[i], eta_below, jnp.maximum(grounds[i], below))
            new = jnp.where(masks[i], new, old)
            f[pl.ds(s + r, SUB), :] = new
            above = f[pl.ds(s + r - 1, SUB), :]
            moved = depths[i] + time_step * (above - new + before[i] - cols[i])
            d[pl.ds(s + r, SUB), :] = jnp.where(masks[i], moved, depths[i])

    def inner(b, carry):
        block(b, active)
        return carry

    for _ in range(STEPS):
        if row0 == 0:
            block(1, top_active)
        lax.fori_loop(2, last, inner, 0)
        block(last, bottom_active)

    span = MAX_BLOCKS * BLOCK
    state = (d, f, c)
    copies = []
    for a, src in enumerate(state):
        if kind == "all":
            for i, slab in enumerate(cs[:-1]):
                copies.append(pltpu.make_async_copy(
                    src.at[pl.ds(i * high + 16, rows)], outs[a].at[:, pl.ds(slab * LANES, LANES)], out_sem.at[a, i]))
                copies[-1].start()
            continue
        for k in range(MAX_BLOCKS):
            keep = k >= MAX_BLOCKS - shift[0, 0]
            if kind == "cols":
                pieces = [(src.at[pl.ds((n - 1 - MAX_BLOCKS + k) * high + 16, rows)], zero,
                           outs[0].at[a, :, pl.ds(k * BLOCK, BLOCK)], k)]
            else:
                pieces = [(src.at[pl.ds(i * high + high - 16 - span + k * BLOCK, BLOCK)], zero,
                           outs[0].at[a, pl.ds(k * BLOCK, BLOCK), pl.ds(slab * LANES, LANES)], k * n + i)
                          for i, slab in enumerate(cs[:-1])]
            for data, empty, dst, m in pieces:
                copy = pltpu.make_async_copy(data, dst, out_sem.at[a, m])
                hole = pltpu.make_async_copy(empty, dst, out_sem.at[a, m])
                pl.when(keep)(copy.start)
                pl.when(jnp.logical_not(keep))(hole.start)
                copies.append(copy)
    for copy in copies:
        copy.wait()


def steps_call(kind, args):
    rows, width = args[0].shape
    slabs = width // LANES
    cs, row0 = list(range(slabs + 1)), 0
    span = MAX_BLOCKS * BLOCK
    if kind == "cols":
        cs = cs[slabs - MAX_BLOCKS - 1:]
        out = [jax.ShapeDtypeStruct((3, rows, span), jnp.float32)]
        zero, sems = (rows, LANES), MAX_BLOCKS
    elif kind == "rows":
        row0 = rows - span - SUB
        out = [jax.ShapeDtypeStruct((3, span, width), jnp.float32)]
        zero, sems = (BLOCK, LANES), MAX_BLOCKS * len(cs)
    else:
        out = [jax.ShapeDtypeStruct((rows, width), jnp.float32)] * 3
        zero, sems = (SUB, LANES), len(cs)
    n, high = len(cs), rows - row0 + 32
    anywhere = pl.BlockSpec(memory_space=pl.ANY)
    vmem = pl.BlockSpec(memory_space=pltpu.VMEM)
    smem = pl.BlockSpec(memory_space=pltpu.SMEM)
    buffer = pltpu.VMEM((n * high, LANES), jnp.float32)
    cells = n * high * LANES
    return pl.pallas_call(
        functools.partial(steps_kernel, cs, row0, rows, kind),
        out_shape=out,
        in_specs=[anywhere] * 4 + [vmem, vmem, anywhere, smem, smem],
        out_specs=[anywhere] * len(out),
        scratch_shapes=[buffer] * 4 + [pltpu.VMEM((high, LANES), jnp.float32), buffer, pltpu.VMEM(zero, jnp.float32),
                                       pltpu.SemaphoreType.DMA((4, n)), pltpu.SemaphoreType.DMA((5,)),
                                       pltpu.SemaphoreType.DMA((3, sems))],
        compiler_params=pltpu.CompilerParams(vmem_limit_bytes=40 << 20),
        cost_estimate=pl.CostEstimate(flops=200 * cells, transcendentals=18 * cells, bytes_accessed=28 * cells),
        name="steps_" + kind,
    )(*args)


def pick_kernel(spots, depth, out, slabs, sem):
    rows, width = depth.shape
    copies = [pltpu.make_async_copy(depth.at[:, pl.ds(i * LANES, LANES)], slabs.at[pl.ds(i * rows, rows)], sem.at[i])
              for i in range(width // LANES)]
    for copy in copies:
        copy.start()
    for copy in copies:
        copy.wait()

    def body(k, carry):
        base = pl.multiple_of(k * 16, 16)
        for j in range(16):
            out[pl.ds(base + j, 1), :] = slabs[pl.ds(spots[base + j], 1), :]
        return carry

    lax.fori_loop(0, out.shape[0] // 16, body, 0)


def pick_rows(spots, depth):
    rows, width = depth.shape
    count = spots.shape[0]
    return pl.pallas_call(
        pick_kernel,
        out_shape=jax.ShapeDtypeStruct((count, LANES), jnp.float32),
        in_specs=[pl.BlockSpec(memory_space=pltpu.SMEM), pl.BlockSpec(memory_space=pl.ANY)],
        out_specs=pl.BlockSpec(memory_space=pltpu.VMEM),
        scratch_shapes=[pltpu.VMEM((rows * width // LANES, LANES), jnp.float32),
                        pltpu.SemaphoreType.DMA((width // LANES,))],
        compiler_params=pltpu.CompilerParams(vmem_limit_bytes=16 << 20),
        cost_estimate=pl.CostEstimate(flops=0, transcendentals=0, bytes_accessed=8 * rows * width),
        name="pick_rows",
    )(spots, depth)


def halos(arrays, wet):
    rows, width = arrays[0].shape
    flag = wet.astype(jnp.float32)
    full = lambda shape: jnp.broadcast_to(flag, shape)
    first = jnp.stack([x[:SUB] for x in arrays] + [full((SUB, width))])
    last = jnp.stack([x[rows - SUB:] for x in arrays] + [full((SUB, width))])
    top = passed_along(last, "row", 1)
    bottom = passed_along(first, "row", -1)

    def columns(start):
        mid = jnp.stack([x[:, start:start + EDGE].T for x in arrays] + [full((EDGE, rows))])
        ends = [jnp.swapaxes(x[:, :, start:start + EDGE], 1, 2) for x in (top, bottom)]
        return jnp.concatenate([ends[0], mid, ends[1]], axis=2)

    left = passed_along(columns(width - EDGE), "col", 1)
    right = passed_along(columns(0), "col", -1)
    gap = jnp.zeros((5, LANES - 2 * EDGE, rows + 2 * SUB), jnp.float32)
    side = jnp.swapaxes(jnp.concatenate([right, gap, left], axis=1), 1, 2)
    return top, bottom, jnp.pad(side, ((0, 0), (SUB, SUB), (0, 0)))


def body(
    depth,
    ground,
    flow_rows,
    flow_cols,
    wet_tiles,
    inlet_cell,
    inlet_node,
    inlet_coef,
    shift_rows,
    shift_cols,
):
    tile_rows, tile_cols = depth.shape
    arrays = (depth, ground, flow_rows, flow_cols)
    top, bottom, side = halos(arrays, wet_tiles[0, 0])
    common = arrays + (top, bottom, side, wet_tiles)
    (edge_cols,) = steps_call("cols", common + (shift_cols,))
    moved_cols = passed_along(edge_cols, "col", 1)
    (edge_rows,) = steps_call("rows", common + (shift_rows,))
    moved_rows = passed_along(edge_rows, "row", 1)
    depth, flow_rows, flow_cols = steps_call("all", common + (shift_rows,))
    devices = lax.axis_size("row") * lax.axis_size("col")
    cells = inlet_cell[0, 0]
    cell_row, cell_col = cells // tile_cols, cells % tile_cols
    picked = pick_rows(cell_col // LANES * tile_rows + cell_row, depth)
    lane = jnp.arange(LANES, dtype=jnp.int32)
    chosen = jnp.sum(jnp.where(lane[None, :] == (cell_col % LANES)[:, None], picked, 0.0), axis=1)
    captured = inlet_coef[0, 0] * jnp.maximum(chosen, 0.0)
    node = inlet_node[0, 0]
    owner = (node // NODE_DEV)[None, :] == jnp.arange(devices, dtype=jnp.int32)[:, None]
    within = (node % NODE_DEV)[None, :] == jnp.arange(NODE_DEV, dtype=jnp.int32)[:, None]
    partial_value = lax.dot_general(
        jnp.where(owner, captured[None, :], 0.0), within.astype(jnp.float32), (((1,), (1,)), ((), ())),
        precision=lax.Precision.HIGHEST)
    node_inflow = lax.psum_scatter(partial_value.reshape(-1), ("row", "col"), scatter_dimension=0, tiled=True)
    return (depth, flow_rows, flow_cols, node_inflow, moved_rows, moved_cols)


def solution(mesh):
    return jax.shard_map(
        body,
        mesh=mesh,
        in_specs=(
            P("row", "col"),
            P("row", "col"),
            P("row", "col"),
            P("row", "col"),
            P("row", "col"),
            P("row", "col", None),
            P("row", "col", None),
            P("row", "col", None),
            P("row", "col"),
            P("row", "col"),
        ),
        out_specs=(
            P("row", "col"),
            P("row", "col"),
            P("row", "col"),
            P(("row", "col")),
            P(None, "row", "col"),
            P(None, "row", "col"),
        ),
        check_vma=False,
    )
```

```python
import functools
import math

import jax
import jax.numpy as jnp
from jax import lax
from jax.experimental import pallas as pl
from jax.experimental.pallas import tpu as pltpu
from jax.sharding import PartitionSpec as P

STEPS = 3
BLOCK = 128
MAX_BLOCKS = 2
NODE_DEV = 64
LANES = 128
SUB = 8
EDGE = 4


gravity = 9.81
time_step = 0.1
friction = 0.0025
depth_floor = 0.25
POWER = -7.0 / (3.0 * math.log(2.0))


def passed_along(value, axis, steps):
    count = lax.axis_size(axis)
    leading, last = (max(0, -steps), min(count, count - steps))
    return lax.ppermute(value, axis, [(source, source + steps) for source in range(leading, last)])


def face_update(flow, eta, eta_next, top_ground):
    face_depth = jnp.maximum(jnp.maximum(eta, eta_next) - top_ground, 0.0)
    floored = jnp.maximum(face_depth, depth_floor)
    root = jnp.exp2(POWER * jnp.log(floored))
    drag = (gravity * time_step * friction) * jnp.abs(flow) * root
    pushed = flow - (gravity * time_step) * face_depth * (eta_next - eta)
    return pushed / (1.0 + drag)


def steps_kernel(cs, row0, rows, kind, group, *refs):
    depth, ground, frow, fcol, top, bottom, side, wet, shift = refs[:9]
    if kind == "all":
        outs, scratch = refs[9:12], refs[12:]
    else:
        if kind == "rows":
            refs = refs[:9] + refs[10:]
        outs, scratch = refs[9:10], refs[10:]
    d, g, f, c, w8, zc, zero, in_sem, out_sem = scratch
    n = len(cs)
    high = rows - row0 + 32
    arrays = ((depth, d), (ground, g), (frow, f), (fcol, c))
    copies = []
    for a, (src, dst) in enumerate(arrays):
        for i, slab in enumerate(cs[:-1]):
            copies.append(pltpu.make_async_copy(
                src.at[pl.ds(row0, rows - row0), pl.ds(slab * LANES, LANES)],
                dst.at[pl.ds(i * high + 16, rows - row0)], in_sem.at[a, i]))
    for copy in copies:
        copy.start()
    blank = jnp.zeros((SUB, LANES), jnp.float32)
    for a, (_, dst) in enumerate(arrays):
        for i in range(n - 1):
            lanes = pl.ds(cs[i] * LANES, LANES)
            dst[pl.ds(i * high, SUB), :] = blank
            dst[pl.ds(i * high + 8, SUB), :] = top[pl.ds(a * SUB, SUB), lanes] if row0 == 0 else blank
            dst[pl.ds(i * high + high - 16, SUB), :] = bottom[pl.ds(a * SUB, SUB), lanes]
            dst[pl.ds(i * high + high - 8, SUB), :] = blank
    mixed = side[pl.ds(row0 + LANES - 16, high), :]
    for a, dst in enumerate((d, g, f, c, w8)):
        base = (n - 1) * high if a < 4 else 0
        dst[pl.ds(base, high), :] = pltpu.roll(mixed, LANES - 8 * a - EDGE, 1)
    if kind != "all":
        zero[...] = jnp.zeros_like(zero)
    for copy in copies:
        copy.wait()

    lane = lax.broadcasted_iota(jnp.int32, (SUB, LANES), 1)
    at_last, at_first = lane == LANES - 1, lane == 0
    at_top = lax.broadcasted_iota(jnp.int32, (SUB, LANES), 0) == 0

    def rightward(vals):
        rolled = [pltpu.roll(v, LANES - 1, 1) for v in vals]
        return [jnp.where(at_last, rolled[(i + 1) % n], rolled[i]) for i in range(n)]

    def leftward(vals):
        rolled = [pltpu.roll(v, 1, 1) for v in vals]
        return [jnp.where(at_first, rolled[(i - 1) % n], rolled[i]) for i in range(n)]

    first = 1 if row0 == 0 else 2
    last = high // SUB - 2
    sizes = [i * high for i in range(n)]

    def bed(b, carry):
        r = pl.multiple_of(b * SUB, SUB)
        vals = [g[pl.ds(s + r, SUB), :] for s in sizes]
        for s, v, q in zip(sizes, vals, rightward(vals)):
            zc[pl.ds(s + r, SUB), :] = jnp.maximum(v, q)
        return carry

    lax.fori_loop(first, last + 1, bed, 0)
    active = jnp.broadcast_to(wet[0, 0], (SUB, LANES)) > 0
    top_active = top[pl.ds(4 * SUB, SUB), pl.ds(0, LANES)] > 0.0
    bottom_active = bottom[pl.ds(4 * SUB, SUB), pl.ds(0, LANES)] > 0.0

    def block(b, count, mask, carry):
        r = b * SUB if isinstance(b, int) else pl.multiple_of(b * SUB, SUB)
        pairs = [(i, j) for j in range(count) for i in range(n)]
        at = {(i, j): sizes[i] + r + j * SUB for i, j in pairs}
        load = lambda ref, off=0: {p: ref[pl.ds(at[p] + off, SUB), :] for p in pairs}
        depths, grounds, depths_below, grounds_below = load(d), load(g), load(d, 1), load(g, 1)
        beds, old_f, old_c = load(zc), load(f), load(c)
        halo = [w8[pl.ds(r + j * SUB, SUB), :] > 0.0 for j in range(count)]
        carry = list(carry)
        done = {}
        for j in range(count):
            masks = [mask] * (n - 1) + [halo[j]]
            eta = [depths[i, j] + grounds[i, j] for i in range(n)]
            right = rightward(eta)
            cols = []
            for i in range(n):
                new = face_update(old_c[i, j], eta[i], right[i], beds[i, j])
                cols.append(jnp.where(masks[i], new, old_c[i, j]))
            before = leftward(cols)
            for i in range(n):
                below = grounds_below[i, j]
                new = face_update(old_f[i, j], eta[i], depths_below[i, j] + below, jnp.maximum(grounds[i, j], below))
                new = jnp.where(masks[i], new, old_f[i, j])
                turned = pltpu.roll(new, 1, 0)
                above = jnp.where(at_top, carry[i], turned)
                carry[i] = turned
                moved = depths[i, j] + time_step * (above - new + before[i] - cols[i])
                done[i, j] = (jnp.where(masks[i], moved, depths[i, j]), new, cols[i])
        for p in pairs:
            for ref, value in zip((d, f, c), done[p]):
                ref[pl.ds(at[p], SUB), :] = value
        return tuple(carry)

    for _ in range(STEPS):
        carry = (blank,) * n
        if row0 == 0:
            carry = block(1, 1, top_active, carry)
        carry = lax.fori_loop(0, (last - 2) // group, lambda k, old: block(k * group + 2, group, active, old), carry)
        block(last, 1, bottom_active, carry)

    span = MAX_BLOCKS * BLOCK
    state = (d, f, c)
    copies = []
    for a, src in enumerate(state):
        if kind == "all":
            for i, slab in enumerate(cs[:-1]):
                copies.append(pltpu.make_async_copy(
                    src.at[pl.ds(i * high + 16, rows)], outs[a].at[:, pl.ds(slab * LANES, LANES)], out_sem.at[a, i]))
                copies[-1].start()
            continue
        for k in range(MAX_BLOCKS):
            keep = k >= MAX_BLOCKS - shift[0, 0]
            if kind == "cols":
                pieces = [(src.at[pl.ds((n - 1 - MAX_BLOCKS + k) * high + 16, rows)], zero,
                           outs[0].at[a, :, pl.ds(k * BLOCK, BLOCK)], k)]
            else:
                pieces = [(src.at[pl.ds(i * high + high - 16 - span + k * BLOCK, BLOCK)], zero,
                           outs[0].at[a, pl.ds(k * BLOCK, BLOCK), pl.ds(slab * LANES, LANES)], k * n + i)
                          for i, slab in enumerate(cs[:-1])]
            for data, empty, dst, m in pieces:
                copy = pltpu.make_async_copy(data, dst, out_sem.at[a, m])
                hole = pltpu.make_async_copy(empty, dst, out_sem.at[a, m])
                pl.when(keep)(copy.start)
                pl.when(jnp.logical_not(keep))(hole.start)
                copies.append(copy)
    for copy in copies:
        copy.wait()


def steps_call(kind, args):
    rows, width = args[0].shape
    slabs = width // LANES
    cs, row0, group = list(range(slabs + 1)), 0, 2
    span = MAX_BLOCKS * BLOCK
    if kind == "cols":
        cs, group = cs[slabs - MAX_BLOCKS - 1:], 4
        out = [jax.ShapeDtypeStruct((3, rows, span), jnp.float32)]
        zero, sems = (rows, LANES), MAX_BLOCKS
    elif kind == "rows":
        row0 = rows - span - 2 * SUB
        out = [jax.ShapeDtypeStruct((3, span, width), jnp.float32)]
        zero, sems = (BLOCK, LANES), MAX_BLOCKS * len(cs)
    else:
        out = [jax.ShapeDtypeStruct((rows, width), jnp.float32)] * 3
        zero, sems = (SUB, LANES), len(cs)
    n, high = len(cs), rows - row0 + 32
    anywhere = pl.BlockSpec(memory_space=pltpu.HBM)
    vmem = pl.BlockSpec(memory_space=pltpu.VMEM)
    smem = pl.BlockSpec(memory_space=pltpu.SMEM)
    buffer = pltpu.VMEM((n * high, LANES), jnp.float32)
    cells = n * high * LANES
    return pl.pallas_call(
        functools.partial(steps_kernel, cs, row0, rows, kind, group),
        out_shape=out,
        in_specs=[anywhere] * 4 + [vmem, vmem, vmem, smem, smem] + [anywhere] * (kind == "rows"),
        out_specs=[anywhere] * len(out),
        scratch_shapes=[buffer] * 4 + [pltpu.VMEM((high, LANES), jnp.float32), buffer, pltpu.VMEM(zero, jnp.float32),
                                       pltpu.SemaphoreType.DMA((4, n)), pltpu.SemaphoreType.DMA((3, sems))],
        compiler_params=pltpu.CompilerParams(vmem_limit_bytes=58 << 20),
        cost_estimate=pl.CostEstimate(flops=cells, transcendentals=0, bytes_accessed=cells),
        name="steps_" + kind,
    )(*args)


def pick_kernel(spots, depth, out, slabs, sem):
    rows, width = depth.shape
    copies = [pltpu.make_async_copy(depth.at[:, pl.ds(i * LANES, LANES)], slabs.at[pl.ds(i * rows, rows)], sem.at[i])
              for i in range(width // LANES)]
    for copy in copies:
        copy.start()
    for copy in copies:
        copy.wait()

    def body(k, carry):
        base = pl.multiple_of(k * 16, 16)
        for j in range(16):
            out[pl.ds(base + j, 1), :] = slabs[pl.ds(spots[base + j], 1), :]
        return carry

    lax.fori_loop(0, out.shape[0] // 16, body, 0)


def pick_rows(spots, depth):
    rows, width = depth.shape
    count = spots.shape[0]
    return pl.pallas_call(
        pick_kernel,
        out_shape=jax.ShapeDtypeStruct((count, LANES), jnp.float32),
        in_specs=[pl.BlockSpec(memory_space=pltpu.SMEM), pl.BlockSpec(memory_space=pltpu.HBM)],
        out_specs=pl.BlockSpec(memory_space=pltpu.VMEM),
        scratch_shapes=[pltpu.VMEM((rows * width // LANES, LANES), jnp.float32),
                        pltpu.SemaphoreType.DMA((width // LANES,))],
        compiler_params=pltpu.CompilerParams(vmem_limit_bytes=58 << 20),
        cost_estimate=pl.CostEstimate(flops=0, transcendentals=0, bytes_accessed=8 * rows * width),
        name="pick_rows",
    )(spots, depth)


def halo_kernel(counts, depth, ground, frow, fcol, wet, top, bottom, side,
                low, high, packed, near, far, got_top, got_bottom, got_left, got_right,
                load_sem, send_sem, recv_sem):
    rows, width = depth.shape
    me_row, me_col = lax.axis_index("row"), lax.axis_index("col")
    moves = [(-1, 0), (1, 0), (0, -1), (0, 1), (-1, -1), (-1, 1), (1, -1), (1, 1)]

    def there(dr, dc):
        r, q = me_row + dr, me_col + dc
        inside = jnp.logical_and(jnp.logical_and(r >= 0, r < counts[0]), jnp.logical_and(q >= 0, q < counts[1]))
        return inside, (r, q)

    for ref in (got_top, got_bottom, got_left, got_right):
        ref[...] = jnp.zeros_like(ref)
    barrier = pltpu.get_barrier_semaphore()
    for move in moves:
        inside, device = there(*move)

        @pl.when(inside)
        def _():
            pl.semaphore_signal(barrier, inc=1, device_id=device, device_id_type=pl.DeviceIdType.MESH)

    copies = []
    for a, src in enumerate((depth, ground, frow, fcol)):
        for k, (piece, dst) in enumerate((
            (src.at[pl.ds(0, SUB), :], near.at[pl.ds(a * SUB, SUB), :]),
            (src.at[pl.ds(rows - SUB, SUB), :], far.at[pl.ds(a * SUB, SUB), :]),
            (src.at[:, pl.ds(0, LANES)], low.at[a]),
            (src.at[:, pl.ds(width - LANES, LANES)], high.at[a]),
        )):
            copies.append(pltpu.make_async_copy(piece, dst, load_sem.at[a, k]))
            copies[-1].start()
    flag = jnp.broadcast_to(wet[0, 0], (SUB, width)).astype(jnp.float32)
    near[pl.ds(4 * SUB, SUB), :] = flag
    far[pl.ds(4 * SUB, SUB), :] = flag
    for copy in copies:
        copy.wait()
    lane = lax.broadcasted_iota(jnp.int32, (LANES, LANES), 1)
    for k in range(rows // LANES):
        part = pl.ds(k * LANES, LANES)
        merged = jnp.broadcast_to(wet[0, 0], (LANES, LANES)).astype(jnp.float32)
        for a in reversed(range(4)):
            ends = jnp.where(lane < LANES // 2, low[a, part, :], high[a, part, :])
            merged = jnp.where(lane < 8 * a + 8, pltpu.roll(ends, 8 * a + EDGE, 1), merged)
        packed[:, part] = merged.T[:5 * SUB, :]

    pl.semaphore_wait(barrier, sum(there(*move)[0].astype(jnp.int32) for move in moves))

    mid = pl.ds(LANES, rows)
    start, end = pl.ds(0, LANES), pl.ds(rows - LANES, LANES)
    above, under = pl.ds(0, LANES), pl.ds(rows + LANES, LANES)
    plan = [
        (near, got_bottom), (far, got_top), (packed, got_right.at[:, mid]), (packed, got_left.at[:, mid]),
        (packed.at[:, start], got_right.at[:, under]), (packed.at[:, start], got_left.at[:, under]),
        (packed.at[:, end], got_right.at[:, above]), (packed.at[:, end], got_left.at[:, above]),
    ]
    sends = []
    for k, (move, (src, dst)) in enumerate(zip(moves, plan)):
        inside, device = there(*move)
        copy = pltpu.make_async_remote_copy(src, dst, send_sem.at[k], recv_sem.at[k], device_id=device,
                                            device_id_type=pl.DeviceIdType.MESH)
        pl.when(inside)(copy.start)
        sends.append((inside, there(-move[0], -move[1])[0], copy))
    for sent, fed, copy in sends:
        pl.when(sent)(copy.wait_send)
        pl.when(fed)(copy.wait_recv)
    top[...] = got_top[...]
    bottom[...] = got_bottom[...]
    from_right = lax.broadcasted_iota(jnp.int32, (5 * SUB, LANES), 0) % SUB >= EDGE
    rest = jnp.zeros((LANES - 5 * SUB, LANES), jnp.float32)
    for k in range(rows // LANES + 2):
        part = pl.ds(k * LANES, LANES)
        both = jnp.where(from_right, got_right[:, part], got_left[:, part])
        side[part, :] = jnp.concatenate([both, rest], axis=0).T


def halos(arrays, wet):
    rows, width = arrays[0].shape
    counts = (lax.axis_size("row"), lax.axis_size("col"))
    across, along = (5 * SUB, width), (5 * SUB, rows + 2 * LANES)
    vmem = lambda shape: pltpu.VMEM(shape, jnp.float32)
    return pl.pallas_call(
        functools.partial(halo_kernel, counts),
        out_shape=[jax.ShapeDtypeStruct(across, jnp.float32)] * 2 + [
            jax.ShapeDtypeStruct((rows + 2 * LANES, LANES), jnp.float32)],
        in_specs=[pl.BlockSpec(memory_space=pltpu.HBM)] * 4 + [pl.BlockSpec(memory_space=pltpu.SMEM)],
        out_specs=[pl.BlockSpec(memory_space=pltpu.VMEM)] * 3,
        scratch_shapes=[vmem((4, rows, LANES)), vmem((4, rows, LANES)), vmem((5 * SUB, rows)), vmem(across), vmem(across),
                        vmem(across), vmem(across), vmem(along), vmem(along),
                        pltpu.SemaphoreType.DMA((4, 4)), pltpu.SemaphoreType.DMA((8,)), pltpu.SemaphoreType.DMA((8,))],
        compiler_params=pltpu.CompilerParams(collective_id=0, has_side_effects=True, vmem_limit_bytes=58 << 20),
        name="halos",
    )(*arrays, wet)


def owners_kernel(counts, parts, total, slots, send_sem, recv_sem):
    n_row, n_col = counts
    devices = n_row * n_col
    me = lax.axis_index("row") * n_col + lax.axis_index("col")
    barrier = pltpu.get_barrier_semaphore()

    def place(k):
        other = lax.rem(me + k, devices)
        return other, (other // n_col, lax.rem(other, n_col))

    @pl.loop(1, devices)
    def _(k):
        pl.semaphore_signal(barrier, inc=1, device_id=place(k)[1], device_id_type=pl.DeviceIdType.MESH)

    pl.semaphore_wait(barrier, devices - 1)

    def send(k):
        other, device = place(k)
        return pltpu.make_async_remote_copy(parts.at[other], slots.at[k], send_sem.at[k], recv_sem.at[k],
                                            device_id=device, device_id_type=pl.DeviceIdType.MESH)

    @pl.loop(1, devices)
    def _(k):
        send(k).start()

    @pl.loop(1, devices)
    def _(k):
        send(k).wait()

    total[...] = parts[me] + jnp.sum(slots[pl.ds(1, devices - 1)], axis=0)


def to_owners(parts):
    counts = (lax.axis_size("row"), lax.axis_size("col"))
    devices = counts[0] * counts[1]
    return pl.pallas_call(
        functools.partial(owners_kernel, counts),
        out_shape=jax.ShapeDtypeStruct((1, LANES), jnp.float32),
        in_specs=[pl.BlockSpec(memory_space=pltpu.VMEM)],
        out_specs=pl.BlockSpec(memory_space=pltpu.VMEM),
        scratch_shapes=[pltpu.VMEM((devices, 1, LANES), jnp.float32), pltpu.SemaphoreType.DMA((devices,)),
                        pltpu.SemaphoreType.DMA((devices,))],
        compiler_params=pltpu.CompilerParams(collective_id=1, has_side_effects=True, vmem_limit_bytes=58 << 20),
        name="to_owners",
    )(parts)


def body(
    depth,
    ground,
    flow_rows,
    flow_cols,
    wet_tiles,
    inlet_cell,
    inlet_node,
    inlet_coef,
    shift_rows,
    shift_cols,
):
    tile_rows, tile_cols = depth.shape
    arrays = (depth, ground, flow_rows, flow_cols)
    top, bottom, side = halos(arrays, wet_tiles)
    common = arrays + (top, bottom, side, wet_tiles)
    (edge_cols,) = steps_call("cols", common + (shift_cols,))
    moved_cols = passed_along(edge_cols, "col", 1)
    (edge_rows,) = steps_call("rows", common + (shift_rows, edge_cols))
    moved_rows = passed_along(edge_rows, "row", 1)
    depth, flow_rows, flow_cols = steps_call("all", common + (shift_rows,))
    devices = lax.axis_size("row") * lax.axis_size("col")
    cells = inlet_cell[0, 0]
    cell_row, cell_col = cells // tile_cols, cells % tile_cols
    picked = pick_rows(cell_col // LANES * tile_rows + cell_row, depth)
    lane = jnp.arange(LANES, dtype=jnp.int32)
    chosen = jnp.sum(jnp.where(lane[None, :] == (cell_col % LANES)[:, None], picked, 0.0), axis=1)
    captured = inlet_coef[0, 0] * jnp.maximum(chosen, 0.0)
    node = inlet_node[0, 0]
    owner = (node // NODE_DEV)[None, :] == jnp.arange(devices, dtype=jnp.int32)[:, None]
    within = (node % NODE_DEV)[None, :] == jnp.arange(LANES, dtype=jnp.int32)[:, None]
    partial_value = lax.dot_general(
        jnp.where(owner, captured[None, :], 0.0), within.astype(jnp.float32), (((1,), (1,)), ((), ())),
        precision=lax.Precision.HIGHEST)
    node_inflow = to_owners(partial_value[:, None, :])[0, :NODE_DEV]
    return (depth, flow_rows, flow_cols, node_inflow, moved_rows, moved_cols)


def solution(mesh):
    return jax.shard_map(
        body,
        mesh=mesh,
        in_specs=(
            P("row", "col"),
            P("row", "col"),
            P("row", "col"),
            P("row", "col"),
            P("row", "col"),
            P("row", "col", None),
            P("row", "col", None),
            P("row", "col", None),
            P("row", "col"),
            P("row", "col"),
        ),
        out_specs=(
            P("row", "col"),
            P("row", "col"),
            P("row", "col"),
            P(("row", "col")),
            P(None, "row", "col"),
            P(None, "row", "col"),
        ),
        check_vma=False,
    )
```

```python
import functools
import math

import jax
import jax.numpy as jnp
from jax import lax
from jax.experimental import pallas as pl
from jax.experimental.pallas import tpu as pltpu
from jax.sharding import PartitionSpec as P

STEPS = 3
BLOCK = 128
MAX_BLOCKS = 2
NODE_DEV = 64
LANES = 128
SUB = 8
EDGE = 4
GROUP = 2


gravity = 9.81
time_step = 0.1
friction = 0.0025
depth_floor = 0.25
POWER = -7.0 / (3.0 * math.log(2.0))


def passed_along(value, axis, steps):
    count = lax.axis_size(axis)
    leading, last = (max(0, -steps), min(count, count - steps))
    return lax.ppermute(value, axis, [(source, source + steps) for source in range(leading, last)])


def face_update(flow, eta, eta_next, top_ground):
    face_depth = jnp.maximum(jnp.maximum(eta, eta_next) - top_ground, 0.0)
    floored = jnp.maximum(face_depth, depth_floor)
    root = jnp.exp2(POWER * jnp.log(floored))
    drag = (gravity * time_step * friction) * jnp.abs(flow) * root
    pushed = flow - (gravity * time_step) * face_depth * (eta_next - eta)
    return pushed * pl.reciprocal(1.0 + drag)


def steps_kernel(cs, rows, group, *refs):
    row0 = 0
    depth, ground, frow, fcol, top, bottom, side, wet, shift_rows, shift_cols = refs[:10]
    outs, edge_rows, edge_cols = refs[10:13], refs[13], refs[14]
    d, g, f, c, w8, zc, zero, in_sem, out_sem, row_sem, col_sem = refs[15:]
    n = len(cs)
    high = rows - row0 + 32
    arrays = ((depth, d), (ground, g), (frow, f), (fcol, c))
    copies = []
    for a, (src, dst) in enumerate(arrays):
        for i, slab in enumerate(cs[:-1]):
            copies.append(pltpu.make_async_copy(
                src.at[pl.ds(row0, rows - row0), pl.ds(slab * LANES, LANES)],
                dst.at[pl.ds(i * high + 16, rows - row0)], in_sem.at[a, i]))
    for copy in copies:
        copy.start()
    blank = jnp.zeros((SUB, LANES), jnp.float32)
    for a, (_, dst) in enumerate(arrays):
        for i in range(n - 1):
            lanes = pl.ds(cs[i] * LANES, LANES)
            dst[pl.ds(i * high, SUB), :] = blank
            dst[pl.ds(i * high + 8, SUB), :] = top[pl.ds(a * SUB, SUB), lanes] if row0 == 0 else blank
            dst[pl.ds(i * high + high - 16, SUB), :] = bottom[pl.ds(a * SUB, SUB), lanes]
            dst[pl.ds(i * high + high - 8, SUB), :] = blank
    mixed = side[pl.ds(row0 + LANES - 16, high), :]
    for a, dst in enumerate((d, g, f, c, w8)):
        base = (n - 1) * high if a < 4 else 0
        dst[pl.ds(base, high), :] = pltpu.roll(mixed, LANES - 8 * a - EDGE, 1)
    zero[...] = jnp.zeros_like(zero)
    for copy in copies:
        copy.wait()

    lane = lax.broadcasted_iota(jnp.int32, (SUB, LANES), 1)
    at_last, at_first = lane == LANES - 1, lane == 0
    at_top = lax.broadcasted_iota(jnp.int32, (SUB, LANES), 0) == 0

    def rightward(vals):
        rolled = [pltpu.roll(v, LANES - 1, 1) for v in vals]
        return [jnp.where(at_last, rolled[(i + 1) % n], rolled[i]) for i in range(n)]

    def leftward(vals):
        rolled = [pltpu.roll(v, 1, 1) for v in vals]
        return [jnp.where(at_first, rolled[(i - 1) % n], rolled[i]) for i in range(n)]

    first = 1 if row0 == 0 else 2
    last = high // SUB - 2
    sizes = [i * high for i in range(n)]

    def bed(b, carry):
        r = pl.multiple_of(b * SUB, SUB)
        vals = [g[pl.ds(s + r, SUB), :] for s in sizes]
        for s, v, q in zip(sizes, vals, rightward(vals)):
            zc[pl.ds(s + r, SUB), :] = jnp.maximum(v, q)
        return carry

    lax.fori_loop(first, last + 1, bed, 0)
    active = jnp.broadcast_to(wet[0, 0], (SUB, LANES)) > 0
    top_active = top[pl.ds(4 * SUB, SUB), pl.ds(0, LANES)] > 0.0
    bottom_active = bottom[pl.ds(4 * SUB, SUB), pl.ds(0, LANES)] > 0.0

    def block(b, count, mask, carry):
        r = b * SUB if isinstance(b, int) else pl.multiple_of(b * SUB, SUB)
        pairs = [(i, j) for j in range(count) for i in range(n)]
        at = {(i, j): sizes[i] + r + j * SUB for i, j in pairs}
        load = lambda ref, off=0: {p: ref[pl.ds(at[p] + off, SUB), :] for p in pairs}
        depths, grounds, depths_below, grounds_below = load(d), load(g), load(d, 1), load(g, 1)
        beds, old_f, old_c = load(zc), load(f), load(c)
        halo = [w8[pl.ds(r + j * SUB, SUB), :] > 0.0 for j in range(count)]
        carry = list(carry)
        done = {}
        for j in range(count):
            masks = [mask] * (n - 1) + [halo[j]]
            eta = [depths[i, j] + grounds[i, j] for i in range(n)]
            right = rightward(eta)
            cols = []
            for i in range(n):
                new = face_update(old_c[i, j], eta[i], right[i], beds[i, j])
                cols.append(jnp.where(masks[i], new, old_c[i, j]))
            before = leftward(cols)
            for i in range(n):
                below = grounds_below[i, j]
                new = face_update(old_f[i, j], eta[i], depths_below[i, j] + below, jnp.maximum(grounds[i, j], below))
                new = jnp.where(masks[i], new, old_f[i, j])
                turned = pltpu.roll(new, 1, 0)
                above = jnp.where(at_top, carry[i], turned)
                carry[i] = turned
                moved = depths[i, j] + time_step * (above - new + before[i] - cols[i])
                done[i, j] = (jnp.where(masks[i], moved, depths[i, j]), new, cols[i])
        for p in pairs:
            for ref, value in zip((d, f, c), done[p]):
                ref[pl.ds(at[p], SUB), :] = value
        return tuple(carry)

    for _ in range(STEPS):
        carry = (blank,) * n
        if row0 == 0:
            carry = block(1, 1, top_active, carry)
        carry = lax.fori_loop(0, (last - 2) // group, lambda k, old: block(k * group + 2, group, active, old), carry)
        block(last, 1, bottom_active, carry)

    span = MAX_BLOCKS * BLOCK
    copies = []

    def hand_on(src, dst, sem, keep):
        copy = pltpu.make_async_copy(src, dst, sem)
        hole = pltpu.make_async_copy(zero.at[pl.ds(0, src.shape[0])], dst, sem)
        pl.when(keep)(copy.start)
        pl.when(jnp.logical_not(keep))(hole.start)
        copies.append(copy)

    for a, src in enumerate((d, f, c)):
        for i, slab in enumerate(cs[:-1]):
            lanes = pl.ds(slab * LANES, LANES)
            copies.append(pltpu.make_async_copy(
                src.at[pl.ds(i * high + 16, rows)], outs[a].at[:, lanes], out_sem.at[a, i]))
            copies[-1].start()
            for k in range(MAX_BLOCKS):
                hand_on(src.at[pl.ds(i * high + high - 16 - span + k * BLOCK, BLOCK)],
                        edge_rows.at[a, pl.ds(k * BLOCK, BLOCK), lanes], row_sem.at[a, k, i],
                        k >= MAX_BLOCKS - shift_rows[0, 0])
        for k in range(MAX_BLOCKS):
            hand_on(src.at[pl.ds((n - 1 - MAX_BLOCKS + k) * high + 16, rows)],
                    edge_cols.at[a, :, pl.ds(k * BLOCK, BLOCK)], col_sem.at[a, k],
                    k >= MAX_BLOCKS - shift_cols[0, 0])
    for copy in copies:
        copy.wait()


def steps_call(*args):
    rows, width = args[0].shape
    span = MAX_BLOCKS * BLOCK
    cs = list(range(width // LANES + 1))
    n, high = len(cs), rows + 32
    anywhere = pl.BlockSpec(memory_space=pltpu.HBM)
    vmem = pl.BlockSpec(memory_space=pltpu.VMEM)
    smem = pl.BlockSpec(memory_space=pltpu.SMEM)
    shapes = [(rows, width)] * 3 + [(3, span, width), (3, rows, span)]
    buffer = pltpu.VMEM((n * high, LANES), jnp.float32)
    return pl.pallas_call(
        functools.partial(steps_kernel, cs, rows, GROUP),
        out_shape=[jax.ShapeDtypeStruct(shape, jnp.float32) for shape in shapes],
        in_specs=[anywhere] * 4 + [vmem] * 3 + [smem] * 3,
        out_specs=[anywhere] * len(shapes),
        scratch_shapes=[buffer] * 4 + [pltpu.VMEM((high, LANES), jnp.float32), buffer,
                                       pltpu.VMEM((rows, LANES), jnp.float32), pltpu.SemaphoreType.DMA((4, n)),
                                       pltpu.SemaphoreType.DMA((3, n)), pltpu.SemaphoreType.DMA((3, MAX_BLOCKS, n)),
                                       pltpu.SemaphoreType.DMA((3, MAX_BLOCKS))],
        compiler_params=pltpu.CompilerParams(vmem_limit_bytes=58 << 20),
        name="steps",
    )(*args)


def pick_kernel(spots, depth, out, slabs, sem):
    rows, width = depth.shape
    copies = [pltpu.make_async_copy(depth.at[:, pl.ds(i * LANES, LANES)], slabs.at[pl.ds(i * rows, rows)], sem.at[i])
              for i in range(width // LANES)]
    for copy in copies:
        copy.start()
    for copy in copies:
        copy.wait()

    def body(k, carry):
        base = pl.multiple_of(k * 16, 16)
        for j in range(16):
            out[pl.ds(base + j, 1), :] = slabs[pl.ds(spots[base + j], 1), :]
        return carry

    lax.fori_loop(0, out.shape[0] // 16, body, 0)


def pick_rows(spots, depth):
    rows, width = depth.shape
    count = spots.shape[0]
    return pl.pallas_call(
        pick_kernel,
        out_shape=jax.ShapeDtypeStruct((count, LANES), jnp.float32),
        in_specs=[pl.BlockSpec(memory_space=pltpu.SMEM), pl.BlockSpec(memory_space=pltpu.HBM)],
        out_specs=pl.BlockSpec(memory_space=pltpu.VMEM),
        scratch_shapes=[pltpu.VMEM((rows * width // LANES, LANES), jnp.float32),
                        pltpu.SemaphoreType.DMA((width // LANES,))],
        compiler_params=pltpu.CompilerParams(vmem_limit_bytes=58 << 20),
        cost_estimate=pl.CostEstimate(flops=0, transcendentals=0, bytes_accessed=rows * width),
        name="pick_rows",
    )(spots, depth)


def halo_kernel(counts, depth, ground, frow, fcol, wet, top, bottom, side,
                low, high, packed, near, far, got_top, got_bottom, got_left, got_right,
                load_sem, send_sem, recv_sem):
    rows, width = depth.shape
    me_row, me_col = lax.axis_index("row"), lax.axis_index("col")
    moves = [(-1, 0), (1, 0), (0, -1), (0, 1), (-1, -1), (-1, 1), (1, -1), (1, 1)]

    def there(dr, dc):
        r, q = me_row + dr, me_col + dc
        inside = jnp.logical_and(jnp.logical_and(r >= 0, r < counts[0]), jnp.logical_and(q >= 0, q < counts[1]))
        return inside, (r, q)

    for ref in (got_top, got_bottom, got_left, got_right):
        ref[...] = jnp.zeros_like(ref)
    barrier = pltpu.get_barrier_semaphore()
    for move in moves:
        inside, device = there(*move)

        @pl.when(inside)
        def _():
            pl.semaphore_signal(barrier, inc=1, device_id=device, device_id_type=pl.DeviceIdType.MESH)

    copies = []
    for a, src in enumerate((depth, ground, frow, fcol)):
        for k, (piece, dst) in enumerate((
            (src.at[pl.ds(0, SUB), :], near.at[pl.ds(a * SUB, SUB), :]),
            (src.at[pl.ds(rows - SUB, SUB), :], far.at[pl.ds(a * SUB, SUB), :]),
            (src.at[:, pl.ds(0, LANES)], low.at[a]),
            (src.at[:, pl.ds(width - LANES, LANES)], high.at[a]),
        )):
            copies.append(pltpu.make_async_copy(piece, dst, load_sem.at[a, k]))
            copies[-1].start()
    flag = jnp.broadcast_to(wet[0, 0], (SUB, width)).astype(jnp.float32)
    near[pl.ds(4 * SUB, SUB), :] = flag
    far[pl.ds(4 * SUB, SUB), :] = flag
    for copy in copies:
        copy.wait()
    lane = lax.broadcasted_iota(jnp.int32, (LANES, LANES), 1)
    for k in range(rows // LANES):
        part = pl.ds(k * LANES, LANES)
        merged = jnp.broadcast_to(wet[0, 0], (LANES, LANES)).astype(jnp.float32)
        for a in reversed(range(4)):
            ends = jnp.where(lane < LANES // 2, low[a, part, :], high[a, part, :])
            merged = jnp.where(lane < 8 * a + 8, pltpu.roll(ends, 8 * a + EDGE, 1), merged)
        packed[:, part] = merged.T[:5 * SUB, :]

    pl.semaphore_wait(barrier, sum(there(*move)[0].astype(jnp.int32) for move in moves))

    mid = pl.ds(LANES, rows)
    start, end = pl.ds(0, LANES), pl.ds(rows - LANES, LANES)
    above, under = pl.ds(0, LANES), pl.ds(rows + LANES, LANES)
    plan = [
        (near, got_bottom), (far, got_top), (packed, got_right.at[:, mid]), (packed, got_left.at[:, mid]),
        (packed.at[:, start], got_right.at[:, under]), (packed.at[:, start], got_left.at[:, under]),
        (packed.at[:, end], got_right.at[:, above]), (packed.at[:, end], got_left.at[:, above]),
    ]
    sends = []
    for k, (move, (src, dst)) in enumerate(zip(moves, plan)):
        inside, device = there(*move)
        copy = pltpu.make_async_remote_copy(src, dst, send_sem.at[k], recv_sem.at[k], device_id=device,
                                            device_id_type=pl.DeviceIdType.MESH)
        pl.when(inside)(copy.start)
        sends.append((inside, there(-move[0], -move[1])[0], copy))
    for sent, fed, copy in sends:
        pl.when(sent)(copy.wait_send)
        pl.when(fed)(copy.wait_recv)
    top[...] = got_top[...]
    bottom[...] = got_bottom[...]
    from_right = lax.broadcasted_iota(jnp.int32, (5 * SUB, LANES), 0) % SUB >= EDGE
    rest = jnp.zeros((LANES - 5 * SUB, LANES), jnp.float32)
    for k in range(rows // LANES + 2):
        part = pl.ds(k * LANES, LANES)
        both = jnp.where(from_right, got_right[:, part], got_left[:, part])
        side[part, :] = jnp.concatenate([both, rest], axis=0).T


def halos(arrays, wet):
    rows, width = arrays[0].shape
    counts = (lax.axis_size("row"), lax.axis_size("col"))
    across, along = (5 * SUB, width), (5 * SUB, rows + 2 * LANES)
    vmem = lambda shape: pltpu.VMEM(shape, jnp.float32)
    return pl.pallas_call(
        functools.partial(halo_kernel, counts),
        out_shape=[jax.ShapeDtypeStruct(across, jnp.float32)] * 2 + [
            jax.ShapeDtypeStruct((rows + 2 * LANES, LANES), jnp.float32)],
        in_specs=[pl.BlockSpec(memory_space=pltpu.HBM)] * 4 + [pl.BlockSpec(memory_space=pltpu.SMEM)],
        out_specs=[pl.BlockSpec(memory_space=pltpu.VMEM)] * 3,
        scratch_shapes=[vmem((4, rows, LANES)), vmem((4, rows, LANES)), vmem((5 * SUB, rows)), vmem(across), vmem(across),
                        vmem(across), vmem(across), vmem(along), vmem(along),
                        pltpu.SemaphoreType.DMA((4, 4)), pltpu.SemaphoreType.DMA((8,)), pltpu.SemaphoreType.DMA((8,))],
        compiler_params=pltpu.CompilerParams(collective_id=0, has_side_effects=True, vmem_limit_bytes=58 << 20),
        name="halos",
    )(*arrays, wet)


def owners_kernel(counts, parts, total, slots, send_sem, recv_sem):
    n_row, n_col = counts
    devices = n_row * n_col
    me = lax.axis_index("row") * n_col + lax.axis_index("col")
    barrier = pltpu.get_barrier_semaphore()

    def place(k):
        other = lax.rem(me + k, devices)
        return other, (other // n_col, lax.rem(other, n_col))

    @pl.loop(1, devices)
    def _(k):
        pl.semaphore_signal(barrier, inc=1, device_id=place(k)[1], device_id_type=pl.DeviceIdType.MESH)

    pl.semaphore_wait(barrier, devices - 1)

    def send(k):
        other, device = place(k)
        return pltpu.make_async_remote_copy(parts.at[other], slots.at[k], send_sem.at[k], recv_sem.at[k],
                                            device_id=device, device_id_type=pl.DeviceIdType.MESH)

    @pl.loop(1, devices)
    def _(k):
        send(k).start()

    @pl.loop(1, devices)
    def _(k):
        send(k).wait()

    total[...] = parts[me] + jnp.sum(slots[pl.ds(1, devices - 1)], axis=0)


def to_owners(parts):
    counts = (lax.axis_size("row"), lax.axis_size("col"))
    devices = counts[0] * counts[1]
    return pl.pallas_call(
        functools.partial(owners_kernel, counts),
        out_shape=jax.ShapeDtypeStruct((1, LANES), jnp.float32),
        in_specs=[pl.BlockSpec(memory_space=pltpu.VMEM)],
        out_specs=pl.BlockSpec(memory_space=pltpu.VMEM),
        scratch_shapes=[pltpu.VMEM((devices, 1, LANES), jnp.float32), pltpu.SemaphoreType.DMA((devices,)),
                        pltpu.SemaphoreType.DMA((devices,))],
        compiler_params=pltpu.CompilerParams(collective_id=1, has_side_effects=True, vmem_limit_bytes=58 << 20),
        name="to_owners",
    )(parts)


def body(
    depth,
    ground,
    flow_rows,
    flow_cols,
    wet_tiles,
    inlet_cell,
    inlet_node,
    inlet_coef,
    shift_rows,
    shift_cols,
):
    tile_rows, tile_cols = depth.shape
    arrays = (depth, ground, flow_rows, flow_cols)
    top, bottom, side = halos(arrays, wet_tiles)
    depth, flow_rows, flow_cols, edge_rows, edge_cols = steps_call(
        *arrays, top, bottom, side, wet_tiles, shift_rows, shift_cols)
    moved_cols = passed_along(edge_cols, "col", 1)
    moved_rows = passed_along(edge_rows, "row", 1)
    devices = lax.axis_size("row") * lax.axis_size("col")
    cells = inlet_cell[0, 0]
    cell_row, cell_col = cells // tile_cols, cells % tile_cols
    picked = pick_rows(cell_col // LANES * tile_rows + cell_row, depth)
    lane = jnp.arange(LANES, dtype=jnp.int32)
    chosen = jnp.sum(jnp.where(lane[None, :] == (cell_col % LANES)[:, None], picked, 0.0), axis=1)
    captured = inlet_coef[0, 0] * jnp.maximum(chosen, 0.0)
    node = inlet_node[0, 0]
    owner = (node // NODE_DEV)[None, :] == jnp.arange(devices, dtype=jnp.int32)[:, None]
    within = (node % NODE_DEV)[None, :] == jnp.arange(LANES, dtype=jnp.int32)[:, None]
    partial_value = lax.dot_general(
        jnp.where(owner, captured[None, :], 0.0), within.astype(jnp.float32), (((1,), (1,)), ((), ())),
        precision=lax.Precision.HIGHEST)
    node_inflow = to_owners(partial_value[:, None, :])[0, :NODE_DEV]
    return (depth, flow_rows, flow_cols, node_inflow, moved_rows, moved_cols)


def solution(mesh):
    return jax.shard_map(
        body,
        mesh=mesh,
        in_specs=(
            P("row", "col"),
            P("row", "col"),
            P("row", "col"),
            P("row", "col"),
            P("row", "col"),
            P("row", "col", None),
            P("row", "col", None),
            P("row", "col", None),
            P("row", "col"),
            P("row", "col"),
        ),
        out_specs=(
            P("row", "col"),
            P("row", "col"),
            P("row", "col"),
            P(("row", "col")),
            P(None, "row", "col"),
            P(None, "row", "col"),
        ),
        check_vma=False,
    )
```
